32 devices in a mesh: dp: 16 (over z, y, x), seq: 2 (over core).
Axes of the slice: x: 2, y: 2, z: 4, core: 2. Of those that a mesh axis runs over, the one named last changes fastest.
Arguments:
- layer_input: bfloat16 [16, 256, 1088], P('dp', 'seq'), may hold values from -6 to 6
- segments: int32 [16, 256], P('dp'), may hold values from 0 to 3, never falling along the last dimension, each value on 1 to 128 neighbouring positions
- w_attn: bfloat16 [3551232], P(('dp', 'seq')), may hold values from -1 to 1
- w_out: bfloat16 [1183744], P(('dp', 'seq')), may hold values from -1.5 to 1.5
- w_fc: bfloat16 [4734976], P(('dp', 'seq')), may hold values from -0.1875 to 0.1875
- w_proj: bfloat16 [4734976], P(('dp', 'seq')), may hold values from -0.09375 to 0.09375
- norm_params: bfloat16 [4352], P(('dp', 'seq')), may hold values from -1 to 3
- lin_bias: bfloat16 [4352], P(('dp', 'seq')), may hold values from -3 to 3
- fc_bias: bfloat16 [4352], P(('dp', 'seq')), may hold values from -3 to 3
- out_cotangent: bfloat16 [16, 256, 1088], P('dp', 'seq'), may hold values from -6 to 6
Outputs:
- layer_output: bfloat16 [16, 256, 1088], P('dp', 'seq')
- input_grad: float32 [16, 256, 1088], P('dp', 'seq')
- w_attn_grad: float32 [3551232], P(('dp', 'seq'))
- w_out_grad: float32 [1183744], P(('dp', 'seq'))
- w_fc_grad: float32 [4734976], P(('dp', 'seq'))
- w_proj_grad: float32 [4734976], P(('dp', 'seq'))
- norm_grad: float32 [4352], P(('dp', 'seq'))
- bias_grad: float32 [4352], P(('dp', 'seq'))
- fc_bias_grad: float32 [4352], P(('dp', 'seq'))
The draws below stay inside these ranges and needn't reach their ends.
Inputs may be any that keep to these rules, and one draw needn't show every extreme that they name: `segments`: along each sequence the numbers never fall; each number marks one document.
All inputs are finite; a program needn't handle non-finite values.
Results may differ from the reference program's by a relative error of at most 0.011.
Values may be sent and summed in bfloat16 or wider, within the bound.
A program may use at most 320 MiB of HBM per device.

```python
import math
import jax
import jax.numpy as jnp
import numpy as np
from jax import lax

D = 1088
H = 17
HD = 64
FF = 4352
SEQLEN = 256
SEQS = 16


def draw_w_attn(key, part):
    base_key = jax.random.fold_in(key, 11)
    matrix = jnp.clip(jax.random.normal(base_key, (D, 3 * D), jnp.float32), -6.0, 6.0) * D ** (-0.5)
    return jnp.clip(matrix, -1.0, 1.0).reshape(-1).astype(jnp.bfloat16)


def draw_norm_params(key, part):
    gain_key = jax.random.fold_in(key, 21)
    offset_key = jax.random.fold_in(key, 22)
    gains = jax.random.uniform(gain_key, (2, 1, D), jnp.float32, 0.5, 1.5)
    offsets = jnp.clip(0.3 * jax.random.normal(offset_key, (2, 1, D), jnp.float32), -1.0, 1.0)
    return jnp.concatenate([gains, offsets], axis=1).reshape(-1).astype(jnp.bfloat16)


def shard_levels(key, extent, cuts, low, high):
    gain, own = 1.0, jax.random.fold_in(key, 6)
    for dim, shards_of in cuts:
        steps = jnp.exp(jax.random.uniform(jax.random.fold_in(own, dim), (shards_of,), jnp.float32, low / len(cuts), high / len(cuts)))
        gain = gain * jnp.repeat(steps, extent[dim] // shards_of).reshape([-1 if axis == dim else 1 for axis in range(len(extent))])
    return gain


def profile(number_of, total, reach, lean):
    weights = [(1 << 20) // math.isqrt(grade ** lean) + 1 for grade in range(2, number_of + 1)]
    surplus, holding = total - reach - (number_of - 1), [1] * (number_of - 1)
    while surplus > 0:
        candidates = [i for i in range(number_of - 1) if holding[i] < reach]
        mass, remaining = sum([weights[i] for i in candidates]), surplus
        for i in candidates:
            addition = min(reach - holding[i], max(1, remaining * weights[i] // mass), surplus)
            holding[i] = holding[i] + addition
            surplus = surplus - addition
    return np.array([reach] + holding)


def ragged(rng, number_of, total, most, lean):
    if number_of == 2:
        one = jax.random.randint(rng, (), max(1, total - most), min(most, total - 1) + 1)
        return jnp.stack([one, total - one])
    sizes = jnp.asarray(profile(number_of, total, most, lean), jnp.int32)
    pairs = (number_of - 1) // 2
    giver, sink = sizes[1:1 + 2 * pairs:2], sizes[2:2 + 2 * pairs:2]
    slack = jnp.minimum(giver - 1, most - sink)
    passed = jax.random.randint(jax.random.fold_in(rng, 1), (pairs,), 0, 1 << 20) % (slack + 1)
    sizes = sizes.at[1:1 + 2 * pairs:2].set(giver - passed).at[2:2 + 2 * pairs:2].set(sink + passed)
    return sizes[jax.random.permutation(jax.random.fold_in(rng, 2), number_of)]


def scatter_about(key, dims, spread, bound, pieces=(), dtype=jnp.bfloat16):
    entries = jax.random.normal(key, dims, jnp.float32) * spread
    if len(pieces) > 0:
        entries = shard_levels(key, dims, pieces, -0.22, 0.18) * entries
    return jnp.clip(entries, min=-bound, max=bound).astype(dtype)


def setup_inputs(seed: int = 0) -> dict:
    key_of = jax.random.split(jax.random.key(seed), 11)
    return {
        "layer_input": scatter_about(key_of[0], (SEQS, SEQLEN, D), 1.0, 6.0, ((0, 16), (1, 2))),
        "segments": jax.vmap(lambda own: jnp.searchsorted(jnp.cumsum(ragged(own, 4, SEQLEN, SEQLEN // 2, 0)), jnp.arange(SEQLEN), side="right"))(jax.random.split(key_of[1], SEQS)).reshape((SEQS, SEQLEN)).astype(jnp.int32),
        "w_attn": draw_w_attn(jax.random.fold_in(key_of[10], 71), 0),
        "w_out": scatter_about(key_of[3], (D * D,), (D // 64) ** -0.5, 1.5, ((0, 32),)),
        "w_fc": scatter_about(key_of[4], (D * FF,), D ** -0.5, 0.1875, ((0, 32),)),
        "w_proj": scatter_about(key_of[5], (FF * D,), FF ** -0.5, 0.09375, ((0, 32),)),
        "norm_params": draw_norm_params(jax.random.fold_in(key_of[10], 71), 0),
        "lin_bias": scatter_about(key_of[7], (4 * D,), 0.3, 3.0, ((0, 32),)),
        "fc_bias": scatter_about(key_of[8], (FF,), 0.3, 3.0, ((0, 32),)),
        "out_cotangent": scatter_about(key_of[9], (SEQS, SEQLEN, D), 1.0, 6.0, ((0, 16), (1, 2))),
    }


GELU_C = 0.7978845608028654
NORM_EPS = 1e-05

def gelu_parts(inputs):
    tanh_value = jnp.tanh(GELU_C * (inputs + 0.044715 * inputs * inputs * inputs))
    value = 0.5 * inputs * (1.0 + tanh_value)
    slope = 0.5 * (1.0 + tanh_value) + 0.5 * inputs * (1.0 - tanh_value * tanh_value) * GELU_C * (1.0 + 3.0 * 0.044715 * inputs * inputs)
    return (value, slope)

def layer_norm(inputs, gains, offsets):
    average = lax.optimization_barrier(jnp.mean(inputs, axis=-1, keepdims=True))
    centred = inputs - average
    inv_std = lax.rsqrt(lax.optimization_barrier(jnp.mean(centred * centred, axis=-1, keepdims=True)) + NORM_EPS)
    x_hat = centred * inv_std
    return (x_hat * gains + offsets, x_hat, inv_std)

def norm_back(grad_out, x_hat, inv_std, gains):
    grad_hat = grad_out * gains
    grad_in = inv_std * (grad_hat - lax.optimization_barrier(jnp.mean(grad_hat, axis=-1, keepdims=True)) - x_hat * lax.optimization_barrier(jnp.mean(grad_hat * x_hat, axis=-1, keepdims=True)))
    return (grad_in, lax.optimization_barrier(jnp.sum(grad_out * x_hat, axis=0)), lax.optimization_barrier(jnp.sum(grad_out, axis=0)))

def score_block(queries, key_rows, allowed):
    scores = jnp.einsum('qhd,khd->hqk', queries.astype(jnp.float32), key_rows.astype(jnp.float32)) * HD ** (-0.5)
    return jnp.where(allowed[None], scores, -1e+30)

def one_sequence(seq_input, seq_segments, seq_cotangent, mats):
    w_qkv, w_o, w_up, w_down, norms, biases, up_bias = mats
    length = seq_input.shape[0]
    inputs_f = seq_input.astype(jnp.float32)
    normed1, x_hat1, inv_std1 = layer_norm(inputs_f, norms[0], norms[1])
    act_in1 = normed1.astype(jnp.bfloat16)
    projected = jnp.dot(act_in1, w_qkv, preferred_element_type=jnp.float32)
    queries = (projected[:, :D] + biases[0]).astype(jnp.bfloat16).reshape(length, H, HD)
    key_rows = projected[:, D:2 * D].astype(jnp.bfloat16).reshape(length, H, HD)
    value_rows = (projected[:, 2 * D:] + biases[1]).astype(jnp.bfloat16).reshape(length, H, HD)
    positions = jnp.arange(length)
    allowed = (positions[None, :] <= positions[:, None]) & (seq_segments[None, :] == seq_segments[:, None])
    scores = score_block(queries, key_rows, allowed)
    top_score = lax.optimization_barrier(jnp.max(scores, axis=-1, keepdims=True))
    log_total = top_score + jnp.log(lax.optimization_barrier(jnp.sum(jnp.exp(scores - top_score), axis=-1, keepdims=True)))
    attn_probs = jnp.exp(scores - log_total).astype(jnp.bfloat16)
    attended = jnp.einsum('hqk,khd->qhd', attn_probs.astype(jnp.float32), value_rows.astype(jnp.float32))
    attended = attended.reshape(length, D).astype(jnp.bfloat16)
    resid = inputs_f + jnp.dot(attended, w_o, preferred_element_type=jnp.float32) + biases[2]
    normed2, x_hat2, inv_std2 = layer_norm(resid, norms[2], norms[3])
    act_in2 = normed2.astype(jnp.bfloat16)
    hidden_pre = jnp.dot(act_in2, w_up, preferred_element_type=jnp.float32) + up_bias
    hidden_act, hidden_slope = gelu_parts(hidden_pre)
    hidden_b = hidden_act.astype(jnp.bfloat16)
    result = (resid + jnp.dot(hidden_b, w_down, preferred_element_type=jnp.float32) + biases[3]).astype(jnp.bfloat16)
    grad_out = seq_cotangent.astype(jnp.float32)
    grad_down = jnp.dot(hidden_b.T, seq_cotangent, preferred_element_type=jnp.float32)
    grad_bp = lax.optimization_barrier(jnp.sum(grad_out, axis=0))
    grad_hidden = jnp.dot(seq_cotangent, w_down.T, preferred_element_type=jnp.float32) * hidden_slope
    grad_hidden_b = grad_hidden.astype(jnp.bfloat16)
    grad_up = jnp.dot(act_in2.T, grad_hidden_b, preferred_element_type=jnp.float32)
    grad_up_bias = lax.optimization_barrier(jnp.sum(grad_hidden, axis=0))
    grad_norm2 = jnp.dot(grad_hidden_b, w_up.T, preferred_element_type=jnp.float32)
    grad_resid_n, grad_g2, grad_b2 = norm_back(grad_norm2, x_hat2, inv_std2, norms[2])
    grad_resid = grad_out + grad_resid_n
    grad_resid_b = grad_resid.astype(jnp.bfloat16)
    grad_o = jnp.dot(attended.T, grad_resid_b, preferred_element_type=jnp.float32)
    grad_bo = lax.optimization_barrier(jnp.sum(grad_resid, axis=0))
    grad_att = jnp.dot(grad_resid_b, w_o.T, preferred_element_type=jnp.float32).astype(jnp.bfloat16).reshape(length, H, HD)
    probs_full = jnp.exp(score_block(queries, key_rows, allowed) - log_total)
    probs_b = probs_full.astype(jnp.bfloat16)
    grad_probs = jnp.einsum('qhd,khd->hqk', grad_att.astype(jnp.float32), value_rows.astype(jnp.float32))
    delta = lax.optimization_barrier(jnp.sum(probs_full * grad_probs, axis=-1, keepdims=True))
    grad_scores = (probs_full * (grad_probs - delta) * HD ** (-0.5)).astype(jnp.bfloat16).astype(jnp.float32)
    grad_q = jnp.einsum('hqk,khd->qhd', grad_scores, key_rows.astype(jnp.float32)).reshape(length, D)
    grad_k = jnp.einsum('hqk,qhd->khd', grad_scores, queries.astype(jnp.float32)).reshape(length, D)
    grad_v = jnp.einsum('hqk,qhd->khd', probs_b.astype(jnp.float32), grad_att.astype(jnp.float32)).reshape(length, D)
    grad_proj_b = jnp.concatenate([grad_q, grad_k, grad_v], axis=1).astype(jnp.bfloat16)
    grad_qkv = jnp.dot(act_in1.T, grad_proj_b, preferred_element_type=jnp.float32)
    grad_norm1 = jnp.dot(grad_proj_b, w_qkv.T, preferred_element_type=jnp.float32)
    grad_in_n, grad_g1, grad_b1 = norm_back(grad_norm1, x_hat1, inv_std1, norms[0])
    grad_input = grad_resid + grad_in_n
    norm_terms = jnp.stack([grad_g1, grad_b1, grad_g2, grad_b2])
    bias_terms = jnp.stack([lax.optimization_barrier(jnp.sum(grad_q, axis=0)), lax.optimization_barrier(jnp.sum(grad_v, axis=0)), grad_bo, grad_bp])
    grads = (grad_qkv, grad_o, grad_up, grad_down, norm_terms, bias_terms, grad_up_bias)
    return (result, grad_input, grads)

def reference(layer_input, segments, w_attn, w_out, w_fc, w_proj, norm_params, lin_bias, fc_bias, out_cotangent):
    mats = (w_attn.reshape(D, 3 * D), w_out.reshape(D, D), w_fc.reshape(D, FF), w_proj.reshape(FF, D), norm_params.astype(jnp.float32).reshape(4, D), lin_bias.astype(jnp.float32).reshape(4, D), fc_bias.astype(jnp.float32))
    zeros = (jnp.zeros((D, 3 * D), jnp.float32), jnp.zeros((D, D), jnp.float32), jnp.zeros((D, FF), jnp.float32), jnp.zeros((FF, D), jnp.float32), jnp.zeros((4, D), jnp.float32), jnp.zeros((4, D), jnp.float32), jnp.zeros((FF,), jnp.float32))

    def scan_body(running, inputs):
        result, grad_input, grads = one_sequence(inputs[0], inputs[1], inputs[2], mats)
        return (tuple((total + term for total, term in zip(running, grads))), (result, grad_input))
    totals, stacked = lax.scan(scan_body, zeros, (layer_input, segments, out_cotangent))
    return (stacked[0], stacked[1], totals[0].reshape(-1), totals[1].reshape(-1), totals[2].reshape(-1), totals[3].reshape(-1), totals[4].reshape(-1), totals[5].reshape(-1), totals[6])
```

```python
import jax
import jax.numpy as jnp
from jax import lax
from jax.sharding import PartitionSpec as P

HD = 64
FF = 4352


GELU_C = 0.7978845608028654
NORM_EPS = 1e-05


def gelu_parts(inputs):
    tanh_value = jnp.tanh(GELU_C * (inputs + 0.044715 * inputs * inputs * inputs))
    value = 0.5 * inputs * (1.0 + tanh_value)
    slope = 0.5 * (1.0 + tanh_value) + 0.5 * inputs * (1.0 - tanh_value * tanh_value) * GELU_C * (
        1.0 + 3.0 * 0.044715 * inputs * inputs
    )
    return (value, slope)


def layer_norm(inputs, gains, offsets):
    average = jnp.mean(inputs, axis=-1, keepdims=True)
    centred = inputs - average
    inv_std = lax.rsqrt(jnp.mean(centred * centred, axis=-1, keepdims=True) + NORM_EPS)
    x_hat = centred * inv_std
    return (x_hat * gains + offsets, x_hat, inv_std)


def norm_back(grad_out, x_hat, inv_std, gains):
    grad_hat = grad_out * gains
    grad_in = inv_std * (
        grad_hat
        - jnp.mean(grad_hat, axis=-1, keepdims=True)
        - x_hat * jnp.mean(grad_hat * x_hat, axis=-1, keepdims=True)
    )
    return (grad_in, jnp.sum(grad_out * x_hat, axis=0), jnp.sum(grad_out, axis=0))


def score_block(queries, key_rows, allowed):
    scores = jnp.einsum(
        "qhd,khd->hqk", queries, key_rows, preferred_element_type=jnp.float32
    ) * HD ** (-0.5)
    return jnp.where(allowed[None], scores, -1e30)


def outer_sum(left, right):
    return jnp.einsum("na,nb->ab", left, right, preferred_element_type=jnp.float32)


AXES = ("dp", "seq")


def shard_height(shard, columns):
    size = shard.shape[0]
    return size // columns if size % columns == 0 else 0


def padded(height):
    return -(-height // 8) * 8


def gather_rows(shard, columns, extra=None):
    height = shard_height(shard, columns)
    if not height:
        return lax.all_gather(shard, AXES, axis=0, tiled=True).reshape(-1, columns)
    block = shard.reshape(height, columns)
    room = padded(height) - height
    if extra is not None:
        row = jnp.pad(extra, (0, columns - extra.shape[0]))[None]
        block = jnp.concatenate([block, row], axis=0)
        room -= 1
    if room:
        block = jnp.pad(block, ((0, room), (0, 0)))
    return lax.all_gather(block, AXES, axis=0, tiled=True)


def spread(acts, height):
    room = padded(height) - height
    if not room:
        return acts
    tokens = acts.shape[0]
    parts = acts.reshape(tokens, -1, height)
    return jnp.pad(parts, ((0, 0), (0, 0), (0, room))).reshape(tokens, -1)


def unspread(acts, height):
    if padded(height) == height:
        return acts
    tokens = acts.shape[0]
    return acts.reshape(tokens, -1, padded(height))[:, :, :height].reshape(tokens, -1)


def scatter_rows(blocks, height):
    count = lax.axis_size(AXES)
    sums = lax.psum_scatter(
        blocks.astype(jnp.bfloat16).reshape(count, -1, blocks.shape[-1]),
        AXES,
        scatter_dimension=0,
        tiled=True,
    )[0]
    return sums.astype(jnp.float32)


def scatter_flat(block, shard):
    count = lax.axis_size(AXES)
    return lax.psum_scatter(
        block.reshape(count, shard), AXES, scatter_dimension=0, tiled=True
    )[0]


def per_device(
    layer_input,
    segments,
    w_attn,
    w_out,
    w_fc,
    w_proj,
    norm_params,
    lin_bias,
    fc_bias,
    out_cotangent,
):
    tokens = layer_input.shape[1]
    width = layer_input.shape[2]
    heads = width // HD
    place = lax.axis_index("seq")
    first = place * tokens
    small = norm_params.shape[0]
    height = shard_height(w_attn, 3 * width)
    height = height if shard_height(w_out, width) == height == shard_height(w_fc, FF) else 0
    down_height = shard_height(w_proj, width)
    own_small = jnp.concatenate([norm_params, lin_bias, fc_bias])
    packed = height and padded(height) > height and own_small.shape[0] <= width
    w_qkv = gather_rows(w_attn, 3 * width)
    w_o = gather_rows(w_out, width, own_small if packed else None)
    w_up = gather_rows(w_fc, FF)
    w_down = gather_rows(w_proj, width)
    if packed:
        smalls = w_o.reshape(-1, padded(height), width)[:, height, : 3 * small]
    else:
        smalls = lax.all_gather(own_small, AXES, axis=0)
    smalls = smalls.astype(jnp.float32).reshape(-1, 3, small)
    norms = smalls[:, 0].reshape(4, width)
    biases = smalls[:, 1].reshape(4, width)
    up_bias = smalls[:, 2].reshape(FF)
    inputs_f = layer_input[0].astype(jnp.float32)
    normed1, x_hat1, inv_std1 = layer_norm(inputs_f, norms[0], norms[1])
    act_in1 = normed1.astype(jnp.bfloat16)
    act_rows1 = spread(act_in1, height)
    projected = jnp.dot(act_rows1, w_qkv, preferred_element_type=jnp.float32)
    queries = (projected[:, :width] + biases[0]).astype(jnp.bfloat16)
    own_keys = projected[:, width : 2 * width].astype(jnp.bfloat16)
    own_values = (projected[:, 2 * width :] + biases[1]).astype(jnp.bfloat16)
    key_rows, value_rows = (
        lax.all_gather(own_keys, "seq", axis=0, tiled=True),
        lax.all_gather(own_values, "seq", axis=0, tiled=True),
    )
    key_count = key_rows.shape[0]
    key_pos = jnp.arange(key_count)
    query_pos = first + jnp.arange(tokens)
    padded_seg = jnp.concatenate([jnp.full((tokens,), -1, jnp.int32), segments[0]])
    key_seg = lax.dynamic_slice_in_dim(padded_seg, tokens, key_count)
    query_seg = lax.dynamic_slice_in_dim(segments[0], first, tokens)
    allowed = (key_pos[None, :] <= query_pos[:, None]) & (key_seg[None, :] == query_seg[:, None])
    q_heads = queries.reshape(tokens, heads, HD)
    k_heads = key_rows.reshape(key_count, heads, HD)
    v_heads = value_rows.reshape(key_count, heads, HD)
    scores = score_block(q_heads, k_heads, allowed)
    top_score = jnp.max(scores, axis=-1, keepdims=True)
    log_total = top_score + jnp.log(jnp.sum(jnp.exp(scores - top_score), axis=-1, keepdims=True))
    attn_probs = jnp.exp(scores - log_total).astype(jnp.bfloat16)
    attended = jnp.einsum("hqk,khd->qhd", attn_probs, v_heads, preferred_element_type=jnp.float32)
    attended = attended.reshape(tokens, width).astype(jnp.bfloat16)
    attended_rows = spread(attended, height)
    resid = inputs_f + jnp.dot(attended_rows, w_o, preferred_element_type=jnp.float32) + biases[2]
    normed2, x_hat2, inv_std2 = layer_norm(resid, norms[2], norms[3])
    act_in2 = normed2.astype(jnp.bfloat16)
    act_rows2 = spread(act_in2, height)
    hidden_pre = jnp.dot(act_rows2, w_up, preferred_element_type=jnp.float32) + up_bias
    hidden_act, hidden_slope = gelu_parts(hidden_pre)
    hidden_b = hidden_act.astype(jnp.bfloat16)
    hidden_rows = spread(hidden_b, down_height)
    result = (
        resid + jnp.dot(hidden_rows, w_down, preferred_element_type=jnp.float32) + biases[3]
    ).astype(jnp.bfloat16)
    cotangent = out_cotangent[0]
    grad_out = cotangent.astype(jnp.float32)
    grad_bp = jnp.sum(grad_out, axis=0)
    grad_hidden = (
        unspread(
            jnp.einsum("nd,fd->nf", cotangent, w_down, preferred_element_type=jnp.float32),
            down_height,
        )
        * hidden_slope
    )
    grad_hidden_b = grad_hidden.astype(jnp.bfloat16)
    grad_up_bias = jnp.sum(grad_hidden, axis=0)
    grad_down = outer_sum(hidden_rows, cotangent)
    if down_height:
        proj_sums = scatter_rows(grad_down, down_height)[:down_height].reshape(-1)
    else:
        proj_sums = scatter_flat(grad_down, w_proj.shape[0])
    grad_up = outer_sum(act_rows2, grad_hidden_b)
    if height:
        fc_sums = scatter_rows(grad_up, height)[:height].reshape(-1)
    else:
        fc_sums = scatter_flat(grad_up, w_fc.shape[0])
    grad_norm2 = unspread(
        jnp.einsum("nf,df->nd", grad_hidden_b, w_up, preferred_element_type=jnp.float32), height
    )
    grad_resid_n, grad_g2, grad_b2 = norm_back(grad_norm2, x_hat2, inv_std2, norms[2])
    grad_resid = grad_out + grad_resid_n
    grad_resid_b = grad_resid.astype(jnp.bfloat16)
    grad_bo = jnp.sum(grad_resid, axis=0)
    grad_att = unspread(
        jnp.einsum(
            "ne,de->nd", grad_resid_b, w_o, preferred_element_type=jnp.float32
        ).astype(jnp.bfloat16),
        height,
    )
    grad_att_heads = grad_att.reshape(tokens, heads, HD)
    probs_full = jnp.exp(score_block(q_heads, k_heads, allowed) - log_total)
    probs_b = probs_full.astype(jnp.bfloat16)
    grad_probs = jnp.einsum(
        "qhd,khd->hqk", grad_att_heads, v_heads, preferred_element_type=jnp.float32
    )
    delta = jnp.sum(probs_full * grad_probs, axis=-1, keepdims=True)
    grad_scores = (probs_full * (grad_probs - delta) * HD ** (-0.5)).astype(jnp.bfloat16)
    grad_q = jnp.einsum(
        "hqk,khd->qhd", grad_scores, k_heads, preferred_element_type=jnp.float32
    ).reshape(tokens, width)
    grad_k_all = jnp.einsum(
        "hqk,qhd->khd", grad_scores, q_heads, preferred_element_type=jnp.float32
    ).reshape(key_count, width)
    grad_v_all = jnp.einsum(
        "hqk,qhd->khd", probs_b, grad_att_heads, preferred_element_type=jnp.float32
    ).reshape(key_count, width)
    grad_k, grad_v = (
        lax.psum_scatter(
            grad_k_all.astype(jnp.bfloat16), "seq", scatter_dimension=0, tiled=True
        ).astype(jnp.float32),
        lax.psum_scatter(
            grad_v_all.astype(jnp.bfloat16), "seq", scatter_dimension=0, tiled=True
        ).astype(jnp.float32),
    )
    grad_proj_b = jnp.concatenate([grad_q, grad_k, grad_v], axis=1).astype(jnp.bfloat16)
    grad_norm1 = unspread(
        jnp.einsum("ne,de->nd", grad_proj_b, w_qkv, preferred_element_type=jnp.float32), height
    )
    grad_in_n, grad_g1, grad_b1 = norm_back(grad_norm1, x_hat1, inv_std1, norms[0])
    grad_input = grad_resid + grad_in_n
    norm_terms = jnp.concatenate([grad_g1, grad_b1, grad_g2, grad_b2])
    bias_terms = jnp.concatenate(
        [jnp.sum(grad_q, axis=0), jnp.sum(grad_v, axis=0), grad_bo, grad_bp]
    )
    small_terms = jnp.concatenate(
        [term.reshape(-1, 1, small) for term in (norm_terms, bias_terms, grad_up_bias)], axis=1
    )
    grad_attn = outer_sum(act_rows1, grad_proj_b)
    grad_wo = outer_sum(attended_rows, grad_resid_b)
    if height:
        joined = jnp.concatenate(
            [grad_attn.astype(jnp.bfloat16), grad_wo.astype(jnp.bfloat16)], axis=1
        )
        if packed:
            blocks = joined.reshape(-1, padded(height), 4 * width)
            row = small_terms.astype(jnp.bfloat16).reshape(-1, 1, 3 * small)
            row = jnp.pad(row, ((0, 0), (height, padded(height) - height - 1), (0, width * 4 - 3 * small)))
            joined = (blocks + row).reshape(joined.shape)
        sums = scatter_rows(joined, height)
        qkv_sums = sums[:height, : 3 * width].reshape(-1)
        out_sums = sums[:height, 3 * width :].reshape(-1)
    else:
        qkv_sums = scatter_flat(grad_attn, w_attn.shape[0])
        out_sums = scatter_flat(grad_wo, w_out.shape[0])
    if packed:
        small_sums = sums[height, : 3 * small].reshape(3, small)
    else:
        small_sums = lax.psum_scatter(small_terms, AXES, scatter_dimension=0, tiled=True)[0]
    norm_sums, bias_sums, fcb_sums = small_sums[0], small_sums[1], small_sums[2]
    return (
        result[None],
        grad_input[None],
        qkv_sums,
        out_sums,
        fc_sums,
        proj_sums,
        norm_sums,
        bias_sums,
        fcb_sums,
    )


def solution(mesh):
    return jax.shard_map(
        per_device,
        mesh=mesh,
        in_specs=(
            P("dp", "seq", None),
            P("dp", None),
            P(("dp", "seq")),
            P(("dp", "seq")),
            P(("dp", "seq")),
            P(("dp", "seq")),
            P(("dp", "seq")),
            P(("dp", "seq")),
            P(("dp", "seq")),
            P("dp", "seq", None),
        ),
        out_specs=(
            P("dp", "seq", None),
            P("dp", "seq", None),
            P(("dp", "seq")),
            P(("dp", "seq")),
            P(("dp", "seq")),
            P(("dp", "seq")),
            P(("dp", "seq")),
            P(("dp", "seq")),
            P(("dp", "seq")),
        ),
        check_vma=False,
    )
```

```python
import jax
import jax.numpy as jnp
from jax import lax
from jax.sharding import PartitionSpec as P

HD = 64
FF = 4352


GELU_C = 0.7978845608028654
NORM_EPS = 1e-05


def gelu_parts(inputs):
    tanh_value = jnp.tanh(GELU_C * (inputs + 0.044715 * inputs * inputs * inputs))
    value = 0.5 * inputs * (1.0 + tanh_value)
    slope = 0.5 * (1.0 + tanh_value) + 0.5 * inputs * (1.0 - tanh_value * tanh_value) * GELU_C * (
        1.0 + 3.0 * 0.044715 * inputs * inputs
    )
    return (value, slope)


def layer_norm(inputs, gains, offsets):
    average = jnp.mean(inputs, axis=-1, keepdims=True)
    centred = inputs - average
    inv_std = lax.rsqrt(jnp.mean(centred * centred, axis=-1, keepdims=True) + NORM_EPS)
    x_hat = centred * inv_std
    return (x_hat * gains + offsets, x_hat, inv_std)


def norm_back(grad_out, x_hat, inv_std, gains):
    grad_hat = grad_out * gains
    grad_in = inv_std * (
        grad_hat
        - jnp.mean(grad_hat, axis=-1, keepdims=True)
        - x_hat * jnp.mean(grad_hat * x_hat, axis=-1, keepdims=True)
    )
    return (grad_in, jnp.sum(grad_out * x_hat, axis=0), jnp.sum(grad_out, axis=0))


def score_block(queries, key_rows, allowed):
    scores = jnp.einsum(
        "qhd,khd->hqk", queries, key_rows, preferred_element_type=jnp.float32
    ) * HD ** (-0.5)
    return jnp.where(allowed[None], scores, -1e30)


def outer_sum(left, right):
    return jnp.einsum("na,nb->ab", left, right, preferred_element_type=jnp.float32)


AXES = ("dp", "seq")


def shard_height(shard, columns):
    size = shard.shape[0]
    return size // columns if size % columns == 0 else 0


def tile_height(shard, columns):
    height = shard_height(shard, columns)
    return 0 if height % 8 else height


def padded(height):
    return -(-height // 8) * 8


def gather_rows(shard, columns, height, extra=None):
    if not height:
        return lax.all_gather(shard, AXES, axis=0, tiled=True).reshape(-1, columns)
    block = shard.reshape(height, columns)
    room = padded(height) - height
    if extra is not None:
        row = jnp.pad(extra, (0, columns - extra.shape[0]))[None]
        block = jnp.concatenate([block, row], axis=0)
        room -= 1
    if room:
        block = jnp.pad(block, ((0, room), (0, 0)))
    return lax.all_gather(block, AXES, axis=0, tiled=True)


def spread(acts, height):
    room = padded(height) - height
    if not room:
        return acts
    tokens = acts.shape[0]
    parts = acts.reshape(tokens, -1, height)
    return jnp.pad(parts, ((0, 0), (0, 0), (0, room))).reshape(tokens, -1)


def unspread(acts, height):
    if padded(height) == height:
        return acts
    tokens = acts.shape[0]
    return acts.reshape(tokens, -1, padded(height))[:, :, :height].reshape(tokens, -1)


def scatter_rows(blocks, height):
    count = lax.axis_size(AXES)
    sums = lax.psum_scatter(
        blocks.astype(jnp.bfloat16).reshape(count, -1, blocks.shape[-1]),
        AXES,
        scatter_dimension=0,
        tiled=True,
    )[0]
    return sums.astype(jnp.float32)


def scatter_flat(block, shard):
    count = lax.axis_size(AXES)
    return lax.psum_scatter(
        block.reshape(count, shard), AXES, scatter_dimension=0, tiled=True
    )[0]


def own_half_sum(terms, place, tokens):
    if lax.axis_size("seq") != 2:
        return lax.psum_scatter(
            terms.astype(jnp.bfloat16), "seq", scatter_dimension=0, tiled=True
        ).astype(jnp.float32)
    own = lax.dynamic_slice_in_dim(terms, place * tokens, tokens)
    other = lax.dynamic_slice_in_dim(terms, (1 - place) * tokens, tokens)
    came = lax.ppermute(other.astype(jnp.bfloat16), "seq", [(0, 1), (1, 0)])
    return own + came.astype(jnp.float32)


def per_device(
    layer_input,
    segments,
    w_attn,
    w_out,
    w_fc,
    w_proj,
    norm_params,
    lin_bias,
    fc_bias,
    out_cotangent,
):
    tokens = layer_input.shape[1]
    width = layer_input.shape[2]
    heads = width // HD
    place = lax.axis_index("seq")
    first = place * tokens
    small = norm_params.shape[0]
    height = shard_height(w_attn, 3 * width)
    height = height if shard_height(w_out, width) == height == shard_height(w_fc, FF) else 0
    down_height = tile_height(w_proj, width)
    own_small = jnp.concatenate([norm_params, lin_bias, fc_bias])
    packed = height and padded(height) > height and own_small.shape[0] <= width
    if height:
        lanes = -(-width // 128) * 128
        joined_shard = jnp.concatenate(
            [
                jnp.pad(w_out.reshape(height, width), ((0, 0), (0, lanes - width))),
                w_attn.reshape(height, 3 * width),
            ],
            axis=1,
        ).reshape(-1)
        joined_w = gather_rows(
            joined_shard, lanes + 3 * width, height, own_small if packed else None
        )
        w_o = joined_w[:, :width]
        w_qkv = joined_w[:, lanes:]
    else:
        w_qkv = gather_rows(w_attn, 3 * width, 0)
        w_o = gather_rows(w_out, width, 0)
    w_up = gather_rows(w_fc, FF, height)
    w_down = gather_rows(w_proj, width, down_height)
    if packed:
        smalls = w_o.reshape(-1, padded(height), width)[:, height, : 3 * small]
    else:
        smalls = lax.all_gather(own_small, AXES, axis=0)
    smalls = smalls.astype(jnp.float32).reshape(-1, 3, small)
    norms = smalls[:, 0].reshape(4, width)
    biases = smalls[:, 1].reshape(4, width)
    up_bias = smalls[:, 2].reshape(FF)
    inputs_f = layer_input[0].astype(jnp.float32)
    normed1, x_hat1, inv_std1 = layer_norm(inputs_f, norms[0], norms[1])
    act_in1 = normed1.astype(jnp.bfloat16)
    act_rows1 = spread(act_in1, height)
    projected = jnp.dot(act_rows1, w_qkv, preferred_element_type=jnp.float32)
    queries = (projected[:, :width] + biases[0]).astype(jnp.bfloat16)
    own_keys = projected[:, width : 2 * width].astype(jnp.bfloat16)
    own_values = (projected[:, 2 * width :] + biases[1]).astype(jnp.bfloat16)
    key_rows, value_rows = (
        lax.all_gather(own_keys, "seq", axis=0, tiled=True),
        lax.all_gather(own_values, "seq", axis=0, tiled=True),
    )
    key_count = key_rows.shape[0]
    key_pos = jnp.arange(key_count)
    query_pos = first + jnp.arange(tokens)
    padded_seg = jnp.concatenate([jnp.full((tokens,), -1, jnp.int32), segments[0]])
    key_seg = lax.dynamic_slice_in_dim(padded_seg, tokens, key_count)
    query_seg = lax.dynamic_slice_in_dim(segments[0], first, tokens)
    allowed = (key_pos[None, :] <= query_pos[:, None]) & (key_seg[None, :] == query_seg[:, None])
    q_heads = queries.reshape(tokens, heads, HD)
    k_heads = key_rows.reshape(key_count, heads, HD)
    v_heads = value_rows.reshape(key_count, heads, HD)
    scores = score_block(q_heads, k_heads, allowed)
    top_score = jnp.max(scores, axis=-1, keepdims=True)
    log_total = top_score + jnp.log(jnp.sum(jnp.exp(scores - top_score), axis=-1, keepdims=True))
    attn_probs = jnp.exp(scores - log_total).astype(jnp.bfloat16)
    attended = jnp.einsum("hqk,khd->qhd", attn_probs, v_heads, preferred_element_type=jnp.float32)
    attended = attended.reshape(tokens, width).astype(jnp.bfloat16)
    attended_rows = spread(attended, height)
    resid = inputs_f + jnp.dot(attended_rows, w_o, preferred_element_type=jnp.float32) + biases[2]
    normed2, x_hat2, inv_std2 = layer_norm(resid, norms[2], norms[3])
    act_in2 = normed2.astype(jnp.bfloat16)
    act_rows2 = spread(act_in2, height)
    hidden_pre = jnp.dot(act_rows2, w_up, preferred_element_type=jnp.float32) + up_bias
    hidden_act, hidden_slope = gelu_parts(hidden_pre)
    hidden_b = hidden_act.astype(jnp.bfloat16)
    hidden_rows = spread(hidden_b, down_height)
    result = (
        resid + jnp.dot(hidden_rows, w_down, preferred_element_type=jnp.float32) + biases[3]
    ).astype(jnp.bfloat16)
    cotangent = out_cotangent[0]
    grad_out = cotangent.astype(jnp.float32)
    grad_bp = jnp.sum(grad_out, axis=0)
    grad_hidden = (
        unspread(
            jnp.einsum("nd,fd->nf", cotangent, w_down, preferred_element_type=jnp.float32),
            down_height,
        )
        * hidden_slope
    )
    grad_hidden_b = grad_hidden.astype(jnp.bfloat16)
    grad_down = outer_sum(hidden_rows, cotangent)
    if down_height:
        grad_hidden_b, grad_down = lax.optimization_barrier(
            (grad_hidden_b, grad_down.astype(jnp.bfloat16))
        )
    grad_up_bias = jnp.sum(grad_hidden, axis=0)
    if down_height:
        proj_sums = scatter_rows(grad_down, down_height)[:down_height].reshape(-1)
    else:
        proj_sums = scatter_flat(grad_down, w_proj.shape[0])
    grad_up = outer_sum(act_rows2, grad_hidden_b)
    if height:
        fc_sums = scatter_rows(grad_up, height)[:height].reshape(-1)
    else:
        fc_sums = scatter_flat(grad_up, w_fc.shape[0])
    grad_norm2 = unspread(
        jnp.einsum("nf,df->nd", grad_hidden_b, w_up, preferred_element_type=jnp.float32), height
    )
    grad_resid_n, grad_g2, grad_b2 = norm_back(grad_norm2, x_hat2, inv_std2, norms[2])
    grad_resid = grad_out + grad_resid_n
    grad_resid_b = grad_resid.astype(jnp.bfloat16)
    grad_bo = jnp.sum(grad_resid, axis=0)
    grad_att = unspread(
        jnp.einsum(
            "ne,de->nd", grad_resid_b, w_o, preferred_element_type=jnp.float32
        ).astype(jnp.bfloat16),
        height,
    )
    grad_att_heads = grad_att.reshape(tokens, heads, HD)
    probs_full = jnp.exp(score_block(q_heads, k_heads, allowed) - log_total)
    probs_b = probs_full.astype(jnp.bfloat16)
    grad_probs = jnp.einsum(
        "qhd,khd->hqk", grad_att_heads, v_heads, preferred_element_type=jnp.float32
    )
    delta = jnp.sum(probs_full * grad_probs, axis=-1, keepdims=True)
    grad_scores = (probs_full * (grad_probs - delta) * HD ** (-0.5)).astype(jnp.bfloat16)
    grad_q = jnp.einsum(
        "hqk,khd->qhd", grad_scores, k_heads, preferred_element_type=jnp.float32
    ).reshape(tokens, width)
    grad_k_all = jnp.einsum(
        "hqk,qhd->khd", grad_scores, q_heads, preferred_element_type=jnp.float32
    ).reshape(key_count, width)
    grad_v_all = jnp.einsum(
        "hqk,qhd->khd", probs_b, grad_att_heads, preferred_element_type=jnp.float32
    ).reshape(key_count, width)
    grad_k = own_half_sum(grad_k_all, place, tokens)
    grad_v = own_half_sum(grad_v_all, place, tokens)
    grad_proj_b = jnp.concatenate([grad_q, grad_k, grad_v], axis=1).astype(jnp.bfloat16)
    grad_norm1 = unspread(
        jnp.einsum("ne,de->nd", grad_proj_b, w_qkv, preferred_element_type=jnp.float32), height
    )
    grad_in_n, grad_g1, grad_b1 = norm_back(grad_norm1, x_hat1, inv_std1, norms[0])
    grad_input = grad_resid + grad_in_n
    norm_terms = jnp.concatenate([grad_g1, grad_b1, grad_g2, grad_b2])
    bias_terms = jnp.concatenate(
        [jnp.sum(grad_q, axis=0), jnp.sum(grad_v, axis=0), grad_bo, grad_bp]
    )
    small_terms = jnp.concatenate(
        [term.reshape(-1, 1, small) for term in (norm_terms, bias_terms, grad_up_bias)], axis=1
    )
    grad_attn = outer_sum(act_rows1, grad_proj_b)
    grad_wo = outer_sum(attended_rows, grad_resid_b)
    if height:
        joined = jnp.concatenate(
            [grad_attn.astype(jnp.bfloat16), grad_wo.astype(jnp.bfloat16)], axis=1
        )
        if packed:
            blocks = joined.reshape(-1, padded(height), 4 * width)
            row = small_terms.astype(jnp.bfloat16).reshape(-1, 1, 3 * small)
            row = jnp.pad(row, ((0, 0), (height, padded(height) - height - 1), (0, width * 4 - 3 * small)))
            joined = (blocks + row).reshape(joined.shape)
        sums = scatter_rows(joined, height)
        qkv_sums = sums[:height, : 3 * width].reshape(-1)
        out_sums = sums[:height, 3 * width :].reshape(-1)
    else:
        qkv_sums = scatter_flat(grad_attn, w_attn.shape[0])
        out_sums = scatter_flat(grad_wo, w_out.shape[0])
    if packed:
        small_sums = sums[height, : 3 * small].reshape(3, small)
    else:
        small_sums = lax.psum_scatter(small_terms, AXES, scatter_dimension=0, tiled=True)[0]
    norm_sums, bias_sums, fcb_sums = small_sums[0], small_sums[1], small_sums[2]
    return (
        result[None],
        grad_input[None],
        qkv_sums,
        out_sums,
        fc_sums,
        proj_sums,
        norm_sums,
        bias_sums,
        fcb_sums,
    )


def solution(mesh):
    return jax.shard_map(
        per_device,
        mesh=mesh,
        in_specs=(
            P("dp", "seq", None),
            P("dp", None),
            P(("dp", "seq")),
            P(("dp", "seq")),
            P(("dp", "seq")),
            P(("dp", "seq")),
            P(("dp", "seq")),
            P(("dp", "seq")),
            P(("dp", "seq")),
            P("dp", "seq", None),
        ),
        out_specs=(
            P("dp", "seq", None),
            P("dp", "seq", None),
            P(("dp", "seq")),
            P(("dp", "seq")),
            P(("dp", "seq")),
            P(("dp", "seq")),
            P(("dp", "seq")),
            P(("dp", "seq")),
            P(("dp", "seq")),
        ),
        check_vma=False,
    )
```
